32 devices in a mesh: dp: 8 (over y, x, core), shard: 4 (over z).
Axes of the slice: x: 2, y: 2, z: 4, core: 2. Of those that a mesh axis runs over, the one named last changes fastest.
Arguments:
- gradients: bfloat16 [8, 44, 512, 512], P('dp', 'shard'), may hold values from -60 to 60
- owners: int32 [4, 11], P('shard'), may hold values from 0 to 7, as said below
- block_param: int32 [44], replicated, may hold values from 0 to 6, never falling along the last dimension, each value on 1 to 12 neighbouring positions
- left_stat: float32 [16, 4, 512, 512], P('dp', 'shard'), may hold values from -4 to 8, as said below
- right_stat: float32 [16, 4, 512, 512], P('dp', 'shard'), may hold values from -4 to 8, as said below
- moment: float32 [16, 4, 512, 512], P('dp', 'shard'), may hold values from 0.5 to 50
- left_root: bfloat16 [16, 4, 512, 512], P('dp', 'shard'), may hold values from -1 to 3.5, as said below
- right_root: bfloat16 [16, 4, 512, 512], P('dp', 'shard'), may hold values from -1 to 3.5, as said below
Outputs:
- new_left: float32 [16, 4, 512, 512], P('dp', 'shard')
- new_right: float32 [16, 4, 512, 512], P('dp', 'shard')
- new_moment: float32 [16, 4, 512, 512], P('dp', 'shard')
- update: bfloat16 [44, 512, 512], P('shard')
The draws below stay inside these ranges and needn't reach their ends.
Inputs may be any that keep to these rules, and one draw needn't show every extreme that they name: `owners`: in each row, no value occurs more than 2 times, and some value occurs exactly 2 times. `left_stat`: each slot's matrix is symmetric. `right_stat`: each slot's matrix is symmetric. `left_root`: each slot's matrix is symmetric. `right_root`: each slot's matrix is symmetric.
All inputs are finite; a program needn't handle non-finite values.
Results may differ from the reference program's by a relative error of at most 0.0058.
Values may be sent and summed in bfloat16 or wider, within the bound.
No kernel may reach another device: no remote copies, remote signals or barrier semaphores. Data moves between devices by JAX's collectives and lax.ppermute only.
A program may use at most 192 MiB of HBM per device.

```python
import math
import jax
import jax.numpy as jnp
import numpy as np
from jax import lax

BLOCK = 512
NBLK = 11
CAP = 2
NPARAM = 7
NBLK_ALL = 44
N_DP = 8
N_SHARD = 4


def draw_gradients(key, part):
    noise_key, scale_key = jax.random.split(jax.random.fold_in(key, 11), 2)
    noise = jax.random.normal(noise_key, (N_DP, NBLK_ALL, BLOCK, BLOCK), jnp.float32)
    scales = jnp.exp(jax.random.uniform(scale_key, (1, NBLK_ALL, 1, 1), jnp.float32, math.log(0.075), math.log(0.75))) / math.sqrt(N_DP)
    values = noise * scales
    return jnp.clip(values, -60.0, 60.0).astype(jnp.bfloat16)


def draw_owners(key, part):

    def one_column(column):
        column_key = jax.random.fold_in(key, 101 + column)
        rank_key, first_key, order_key = jax.random.split(column_key, 3)
        ranks = jax.random.permutation(rank_key, N_DP * CAP).astype(jnp.int32)
        doubled = jax.random.randint(first_key, (), 0, N_DP)
        slot_ids = jnp.arange(N_DP * CAP, dtype=jnp.int32)
        ranks = jnp.where(slot_ids // CAP == doubled, slot_ids % CAP - CAP, ranks)
        ordered = jnp.argsort(ranks, stable=True)
        chosen = (ordered[:NBLK] // CAP).astype(jnp.int32)
        return jax.random.permutation(order_key, chosen)
    return jax.vmap(one_column)(jnp.arange(N_SHARD, dtype=jnp.int32)).astype(jnp.int32)


def symmetric_stat(key):
    noise_key, diag_key = jax.random.split(key)
    noise = jax.random.normal(noise_key, (N_DP * CAP, N_SHARD, BLOCK, BLOCK), jnp.float32)
    diagonal = jnp.exp(jax.random.uniform(diag_key, (N_DP * CAP, N_SHARD, BLOCK, 1), jnp.float32, math.log(0.5), math.log(5.0)))
    symmetric = (noise + jnp.swapaxes(noise, -1, -2)) * 0.2
    values = symmetric + diagonal * jnp.eye(BLOCK, dtype=jnp.float32)
    return jnp.clip(values, -4.0, 8.0)


def symmetric_root(key):
    noise_key, diag_key = jax.random.split(key)
    noise = jax.random.normal(noise_key, (N_DP * CAP, N_SHARD, BLOCK, BLOCK), jnp.float32)
    diagonal = jax.random.uniform(diag_key, (N_DP * CAP, N_SHARD, BLOCK, 1), jnp.float32, 1.5, 3.0)
    symmetric = (noise + jnp.swapaxes(noise, -1, -2)) * (0.5 / math.sqrt(2.0 * BLOCK))
    values = symmetric + diagonal * jnp.eye(BLOCK, dtype=jnp.float32)
    return jnp.clip(values, -1.0, 3.5).astype(jnp.bfloat16)


def draw_left_stat(key, part):
    return symmetric_stat(jax.random.fold_in(key, 21))


def draw_right_stat(key, part):
    return symmetric_stat(jax.random.fold_in(key, 22))


def draw_left_root(key, part):
    return symmetric_root(jax.random.fold_in(key, 31))


def draw_right_root(key, part):
    return symmetric_root(jax.random.fold_in(key, 32))


def shard_levels(stream_key, dims, shards, low, top_value):
    def one(axis_at, blocks):
        steps = jax.random.uniform(jax.random.fold_in(jax.random.fold_in(stream_key, 6), axis_at), (blocks,), jnp.float32, low / len(shards), top_value / len(shards))
        return jnp.repeat(jnp.exp(steps), dims[axis_at] // blocks).reshape((-1,) + (1,) * (len(dims) - axis_at - 1))

    factor_of = one(*shards[0])
    for cut in shards[1:]:
        factor_of = factor_of * one(*cut)
    return factor_of


def profile(amount, total, most, slope):
    portions = [(1 << 20) // math.isqrt(rank ** slope) + 1 for rank in range(2, amount + 1)]
    spare, holding = total - most - (amount - 1), [1] * (amount - 1)
    while spare > 0:
        movable = [i for i in range(amount - 1) if holding[i] < most]
        whole, left = sum([portions[i] for i in movable]), spare
        for i in movable:
            addition = min(most - holding[i], max(1, left * portions[i] // whole), spare)
            holding[i] = holding[i] + addition
            spare = spare - addition
    return np.array([most] + holding)


def uneven_parts(rng, count, total, bound, skew):
    if count == 2:
        one = jax.random.randint(rng, (), max(1, total - bound), min(bound, total - 1) + 1)
        return jnp.stack([one, total - one])
    sizes = jnp.asarray(profile(count, total, bound, skew), jnp.int32)
    pairs = (count - 1) // 2
    giver, taker = sizes[1:1 + 2 * pairs:2], sizes[2:2 + 2 * pairs:2]
    slack = jnp.minimum(giver - 1, bound - taker)
    passed = jax.random.randint(jax.random.fold_in(rng, 1), (pairs,), 0, 1 << 20) % (slack + 1)
    sizes = sizes.at[1:1 + 2 * pairs:2].set(giver - passed).at[2:2 + 2 * pairs:2].set(taker + passed)
    return sizes[jax.random.permutation(jax.random.fold_in(rng, 2), count)]


def setup_inputs(seed: int = 0) -> dict:
    streams_of = jax.random.split(jax.random.key(seed), 9)
    return {
        "gradients": draw_gradients(jax.random.fold_in(streams_of[8], 71), 0),
        "owners": draw_owners(jax.random.fold_in(streams_of[8], 71), 0),
        "block_param": jnp.searchsorted(jnp.cumsum(uneven_parts(streams_of[2], NPARAM, NBLK_ALL, 2 * NBLK_ALL // NPARAM, 0)), jnp.arange(NBLK_ALL), side="right").astype(jnp.int32),
        "left_stat": draw_left_stat(jax.random.fold_in(streams_of[8], 71), 0),
        "right_stat": draw_right_stat(jax.random.fold_in(streams_of[8], 71), 0),
        "moment": jnp.clip(jnp.exp(math.log(50.0) - 4.6051702 * jax.random.uniform(streams_of[5], (N_DP * CAP, N_SHARD, BLOCK, BLOCK), jnp.float32) ** shard_levels(streams_of[5], (N_DP * CAP, N_SHARD, BLOCK, BLOCK), ((0, 8), (1, 4)), -0.2, 0.2)), 0.5, 50.0),
        "left_root": draw_left_root(jax.random.fold_in(streams_of[8], 71), 0),
        "right_root": draw_right_root(jax.random.fold_in(streams_of[8], 71), 0),
    }


decay_rate = 0.95
tiny_value = 1e-06

def slot_numbers(owners):
    counter = jnp.arange(owners.shape[1], dtype=jnp.int32)
    same_owner = owners[:, :, None] == owners[:, None, :]
    earlier = counter[None, :] < counter[:, None]
    return lax.optimization_barrier(jnp.sum(jnp.where(same_owner & earlier[None], 1, 0), axis=2)).astype(jnp.int32)

def block_products(operands):
    gradient, left_factor, right_factor = operands
    left_gram = jnp.dot(gradient, gradient.T, precision=lax.Precision.HIGHEST)
    right_gram = jnp.dot(gradient.T, gradient, precision=lax.Precision.HIGHEST)
    left_half = jnp.dot(left_factor, gradient.astype(jnp.bfloat16), preferred_element_type=jnp.float32).astype(jnp.bfloat16)
    direction = jnp.dot(left_half, right_factor, preferred_element_type=jnp.float32)
    return (left_gram, right_gram, direction)

def reference(gradients, owners, block_param, left_stat, right_stat, moment, left_root, right_root):
    summed = lax.optimization_barrier(jnp.sum(gradients, axis=0, dtype=jnp.float32))
    places = owners * CAP + slot_numbers(owners)
    column_ids = jnp.arange(N_SHARD, dtype=jnp.int32)
    left_roots = left_root[places, column_ids[:, None]].reshape(NBLK_ALL, BLOCK, BLOCK)
    right_roots = right_root[places, column_ids[:, None]].reshape(NBLK_ALL, BLOCK, BLOCK)
    left_gram, right_gram, direction = lax.map(block_products, (summed, left_roots, right_roots))
    slot_ids = jnp.arange(N_DP * CAP, dtype=jnp.int32)
    matches = places[:, None, :] == slot_ids[None, :, None]
    is_live = jnp.any(matches, axis=2)
    block_index = lax.optimization_barrier(jnp.sum(jnp.where(matches, jnp.arange(NBLK, dtype=jnp.int32)[None, None, :], 0), axis=2)).astype(jnp.int32)
    flat_index = (column_ids[:, None] * NBLK + block_index).T
    live_mask = is_live.T[:, :, None, None]
    held = jnp.where(live_mask, summed[flat_index], 0.0)
    new_left = decay_rate * left_stat + (1.0 - decay_rate) * jnp.where(live_mask, left_gram[flat_index], 0.0)
    new_right = decay_rate * right_stat + (1.0 - decay_rate) * jnp.where(live_mask, right_gram[flat_index], 0.0)
    new_moment = decay_rate * moment + (1.0 - decay_rate) * held * held
    adam_step = held / (jnp.sqrt(new_moment) + tiny_value)
    adam_squares = lax.optimization_barrier(jnp.sum(adam_step * adam_step, axis=(2, 3)))
    param_ids = jnp.arange(NPARAM, dtype=jnp.int32)
    slot_member = (block_param[flat_index][:, :, None] == param_ids[None, None, :]) & is_live.T[:, :, None]
    adam_norm = lax.optimization_barrier(jnp.sum(jnp.where(slot_member, adam_squares[:, :, None], 0.0), axis=(0, 1)))
    block_member = block_param[:, None] == param_ids[None, :]
    direction_squares = lax.optimization_barrier(jnp.sum(direction * direction, axis=(1, 2)))
    direction_norm = lax.optimization_barrier(jnp.sum(jnp.where(block_member, direction_squares[:, None], 0.0), axis=0))
    graft_ratio = jnp.sqrt((adam_norm + tiny_value) / (direction_norm + tiny_value))
    block_ratio = lax.optimization_barrier(jnp.sum(jnp.where(block_member, graft_ratio[None, :], 0.0), axis=1))
    update = (block_ratio[:, None, None] * direction).astype(jnp.bfloat16)
    return (new_left, new_right, new_moment, update)
```

```python
import functools

import jax
import jax.numpy as jnp
from jax import lax
from jax.experimental import pallas as pl
from jax.experimental.pallas import tpu as pltpu
from jax.sharding import PartitionSpec as P

NPARAM = 7

decay_rate = 0.95
tiny_value = 1e-06

HEAD = 8


def slot_tables(owner_row, params, me, slots, capacity):
    blocks = owner_row.shape[0]

    def kernel(owner_ref, param_ref, me_ref, out_ref, count_ref):
        device = me_ref[0]
        first = me_ref[1] * blocks
        out_ref[0] = device // 4
        out_ref[1] = (device // 2) % 2
        out_ref[2] = device % 2
        for i in range(3, HEAD):
            out_ref[i] = 0
        for s in range(3 * slots):
            out_ref[HEAD + s] = 0
        for s in range(slots // capacity):
            count_ref[s] = 0
        for b in range(blocks):
            owner = owner_ref[b]
            place = owner * capacity + count_ref[owner]
            count_ref[owner] = count_ref[owner] + 1
            out_ref[HEAD + place] = b
            out_ref[HEAD + slots + place] = 1
            out_ref[HEAD + 2 * slots + place] = param_ref[first + b]

    smem = pl.BlockSpec(memory_space=pltpu.SMEM)
    return pl.pallas_call(
        kernel,
        in_specs=[smem, smem, smem],
        out_specs=smem,
        out_shape=jax.ShapeDtypeStruct((HEAD + 3 * slots,), jnp.int32),
        scratch_shapes=[pltpu.SMEM((slots // capacity,), jnp.int32)],
        name="slot_tables",
    )(owner_row, params, me)


def gather_sum(table, sources, count, rows, step, name):
    width = sources[0][0].shape[-1]
    inner = rows // step

    def kernel(t_ref, *refs):
        total = refs[0][...].astype(jnp.float32)
        for ref in refs[1:-1]:
            total = total + ref[...].astype(jnp.float32)
        refs[-1][...] = total.astype(jnp.bfloat16)

    def spec(rule):
        def index(j, i, t):
            block, first = rule(j, t)
            return (block, first * inner + i, 0)

        return pl.BlockSpec((1, step, width), index)

    return pl.pallas_call(
        kernel,
        grid_spec=pltpu.PrefetchScalarGridSpec(
            num_scalar_prefetch=1,
            grid=(count, inner),
            in_specs=[spec(rule) for _, rule in sources],
            out_specs=pl.BlockSpec((1, step, width), lambda j, i, t: (j, i, 0)),
        ),
        out_shape=jax.ShapeDtypeStruct((count, rows, width), jnp.bfloat16),
        name=name,
    )(table, *[array for array, _ in sources])


def on_device(gradients, owners, block_param, left_stat, right_stat, moment, left_root, right_root):
    replicas = lax.axis_size("dp")
    capacity = left_stat.shape[0]
    size = gradients.shape[3]
    half = size // 2
    grads = gradients[0]
    blocks = grads.shape[0]
    slots = replicas * capacity
    lines = replicas // 4
    hops = range(1, lines)

    by_core = [(i, i ^ 1) for i in range(replicas)]
    by_side = [(i, i ^ 2) for i in range(replicas)]

    def by_row(m):
        return [(i, (i + 4 * m) % replicas) for i in range(replicas)]

    def send(array, perm):
        return lax.ppermute(array, "dp", perm)

    me = jnp.stack([lax.axis_index("dp"), lax.axis_index("shard")]).astype(jnp.int32)
    table = slot_tables(owners[0], block_param, me, slots, capacity)

    def row_at(t, m):
        return lax.rem(t[0] + m, lines)

    def block_of(t, row, side, core, k):
        return t[HEAD + ((row * 2 + side) * 2 + core) * capacity + k]

    held = None
    new_moment = None
    tiles = []
    directions = []
    packs, from_core, xs, ys, from_side, from_rows = [], [], [], [], [], []
    for k in range(capacity):
        packs.append(
            gather_sum(
                table,
                [(grads, lambda j, t, k=k: (t[HEAD + (j * 2 + 1 - t[2]) * capacity + k], 0))],
                2 * lines,
                size,
                size,
                f"pack_{k}",
            )
        )
        from_core.append(send(packs[k], by_core))
    for k in range(capacity):
        got = from_core[k]
        xs.append(
            gather_sum(
                table,
                [
                    (grads, lambda j, t, k=k: (block_of(t, j, 1 - t[1], t[2], k), 0)),
                    (got, lambda j, t: (j * 2 + 1 - t[1], 0)),
                ],
                lines,
                half,
                half,
                f"side_part_{k}",
            )
        )
        from_side.append(send(xs[k], by_side))
        ys.append(
            [
                gather_sum(
                    table,
                    [
                        (grads, lambda j, t, k=k, m=m: (block_of(t, row_at(t, m), j, t[2], k), 1)),
                        (got, lambda j, t, m=m: (row_at(t, m) * 2 + j, 1)),
                    ],
                    2,
                    half,
                    half,
                    f"row_part_{k}_{m}",
                )
                for m in hops
            ]
        )
        from_rows.append([send(ys[k][m - 1], by_row(m)) for m in hops])
    rest_rows, rest_side = [], []
    for k in range(capacity):
        got = from_core[k]
        rest_rows.append(
            [
                send(
                    gather_sum(
                        table,
                        [
                            (grads, lambda j, t, k=k, m=m: (block_of(t, row_at(t, m), t[1], t[2], k), 0)),
                            (got, lambda j, t, m=m: (row_at(t, m) * 2 + t[1], 0)),
                            (from_side[k], lambda j, t, m=m: (row_at(t, m), 0)),
                        ],
                        1,
                        half,
                        half // 2,
                        f"row_rest_{k}_{m}",
                    ),
                    by_row(m),
                )
                for m in hops
            ]
        )
        rest_side.append(
            send(
                gather_sum(
                    table,
                    [
                        (grads, lambda j, t, k=k: (block_of(t, t[0], 1 - t[1], t[2], k), 1)),
                        (got, lambda j, t: (t[0] * 2 + 1 - t[1], 1)),
                    ]
                    + [(array, lambda j, t: (1 - t[1], 0)) for array in from_rows[k]],
                    1,
                    half,
                    half // 2,
                    f"side_rest_{k}",
                ),
                by_side,
            )
        )
    for k in range(capacity):
        direction, held, new_moment, tile = owned_slot(
            k,
            capacity,
            slots,
            table,
            grads,
            from_core[k],
            from_side[k],
            from_rows[k],
            rest_rows[k],
            rest_side[k],
            moment,
            left_root,
            right_root,
            held,
            new_moment,
        )
        directions.append(direction)
        tiles.append(tile)

    norms = tiles[0]
    for tile in tiles[1:]:
        norms = norms + tile
    columns = lax.axis_size("shard")
    total = norms
    for shift in range(1, columns):
        total = total + lax.ppermute(
            norms, "shard", [(i, (i + shift) % columns) for i in range(columns)]
        )
    total = total + send(total, by_core)
    total = total + send(total, by_side)
    part = total
    for m in hops:
        total = total + send(part, by_row(m))
    graft_ratio = jnp.sqrt((total[:, 0] + tiny_value) / (total[:, 1] + tiny_value))

    pieces = []
    for k in range(capacity):
        own = directions[k]
        own_s = send(own, by_side)
        own_r = [send(own, by_row(m)) for m in hops]
        far_top = [send(own_s[:half], by_row(m)) for m in hops]
        far_end = [send(array[half:], by_side) for array in own_r]
        near = [(0, 0, (own,)), (0, 1, (own_s,))]
        near += [(m, 0, (own_r[m - 1],)) for m in hops]
        near += [(m, 1, (far_top[m - 1], far_end[m - 1])) for m in hops]
        pieces.append(
            [(m, side, 0, parts) for m, side, parts in near]
            + [(m, side, 1, tuple(send(part, by_core) for part in parts)) for m, side, parts in near]
        )

    left_gram = jnp.einsum("cij,ckj->cik", held, held, precision=lax.Precision.HIGHEST)
    right_gram = jnp.einsum("cji,cjk->cik", held, held, precision=lax.Precision.HIGHEST)
    new_left = decay_rate * left_stat + (1.0 - decay_rate) * left_gram[:, None]
    new_right = decay_rate * right_stat + (1.0 - decay_rate) * right_gram[:, None]

    update = None
    for k in range(capacity):
        update = place_updates(
            k, capacity, slots, lines, table, graft_ratio, pieces[k], update, (blocks, size, size)
        )
    return (new_left, new_right, new_moment, update)


def owned_slot(
    k,
    capacity,
    slots,
    table,
    grads,
    from_core,
    from_side,
    from_rows,
    rest_rows,
    rest_side,
    moment,
    left_root,
    right_root,
    held,
    new_moment,
):
    size = grads.shape[-1]
    half = size // 2
    hops = len(from_rows)
    carried = [] if held is None else [held, new_moment]

    def my_slot(t):
        return ((t[0] * 2 + t[1]) * 2 + t[2]) * capacity + k

    def kernel(t_ref, *refs):
        local, core, side = refs[:3]
        rows_in = refs[3 : 3 + hops]
        rows_rest = refs[3 + hops : 3 + 2 * hops]
        side_rest, moment_ref, left_ref, right_ref = refs[3 + 2 * hops : 7 + 2 * hops]
        direction_ref, held_ref, moment_out, tile_ref = refs[7 + 2 * hops + len(carried) :]
        slot = my_slot(t_ref)
        live = t_ref[HEAD + slots + slot]
        param = t_ref[HEAD + 2 * slots + slot]

        def wide(x):
            return x.astype(jnp.float32)

        both = wide(local[0]) + wide(core[0])
        top = both[:half] + wide(side[0])
        for ref in rows_rest:
            top = top + wide(ref[0])
        end = both[half:] + wide(side_rest[0])
        for ref in rows_in:
            end = end + wide(ref[0])
        summed = jnp.concatenate([top, end], axis=0)
        summed = jnp.where(live > 0, summed, 0.0)
        held_ref[0] = summed
        left_half = jnp.dot(
            left_ref[0, 0], summed.astype(jnp.bfloat16), preferred_element_type=jnp.float32
        ).astype(jnp.bfloat16)
        direction = jnp.dot(left_half, right_ref[0, 0], preferred_element_type=jnp.float32)
        direction_ref[...] = direction.astype(jnp.bfloat16)
        fresh = decay_rate * moment_ref[0, 0] + (1.0 - decay_rate) * (summed * summed)
        moment_out[0, 0] = fresh
        adam = summed / (jnp.sqrt(fresh) + tiny_value)
        adam_square = jnp.sum(adam * adam)
        direction_square = jnp.sum(direction * direction)
        row = lax.broadcasted_iota(jnp.int32, tile_ref.shape, 0)
        lane = lax.broadcasted_iota(jnp.int32, tile_ref.shape, 1)
        value = jnp.where(lane == 0, adam_square, jnp.where(lane == 1, direction_square, 0.0))
        tile_ref[...] = jnp.where((row == param) & (live > 0), value, 0.0)

    half_block = (1, half, size)
    whole = (1, 1, size, size)

    def at_k(i, t):
        return (k, 0, 0, 0)

    in_specs = [
        pl.BlockSpec((1, size, size), lambda i, t: (t[HEAD + my_slot(t)], 0, 0)),
        pl.BlockSpec((1, size, size), lambda i, t: (t[0] * 2 + t[1], 0, 0)),
        pl.BlockSpec(half_block, lambda i, t: (t[0], 0, 0)),
    ]
    in_specs += [pl.BlockSpec(half_block, lambda i, t: (t[1], 0, 0))] * hops
    in_specs += [pl.BlockSpec(half_block, lambda i, t: (0, 0, 0))] * (hops + 1)
    in_specs += [pl.BlockSpec(whole, at_k)] * 3
    in_specs += [pl.BlockSpec(memory_space=pl.ANY)] * len(carried)
    first = 1 + 7 + 2 * hops
    return pl.pallas_call(
        kernel,
        grid_spec=pltpu.PrefetchScalarGridSpec(
            num_scalar_prefetch=1,
            grid=(1,),
            in_specs=in_specs,
            out_specs=[
                pl.BlockSpec((size, size), lambda i, t: (0, 0)),
                pl.BlockSpec((1, size, size), lambda i, t: (k, 0, 0)),
                pl.BlockSpec(whole, at_k),
                pl.BlockSpec((8, 128), lambda i, t: (0, 0)),
            ],
        ),
        out_shape=[
            jax.ShapeDtypeStruct((size, size), jnp.bfloat16),
            jax.ShapeDtypeStruct((capacity, size, size), jnp.float32),
            jax.ShapeDtypeStruct(moment.shape, jnp.float32),
            jax.ShapeDtypeStruct((8, 128), jnp.float32),
        ],
        input_output_aliases={first: 1, first + 1: 2} if carried else {},
        name=f"owned_slot_{k}",
    )(
        table,
        grads,
        from_core,
        from_side,
        *from_rows,
        *rest_rows,
        rest_side,
        moment,
        left_root,
        right_root,
        *carried,
    )


def place_updates(k, capacity, slots, lines, table, graft_ratio, pieces, update, shape):
    size = shape[-1]
    flat = [part for _, _, _, parts in pieces for part in parts]
    carried = [] if update is None else [update]

    def kernel(t_ref, ratio_ref, *refs):
        sources = refs[: len(flat)]
        out_ref, in_buf, out_buf, in_sem, out_sem = refs[len(flat) + len(carried) :]

        def slot_of(m, side, core):
            row = lax.rem(t_ref[0] + lines - m, lines)
            side = t_ref[1] ^ side
            core = t_ref[2] ^ core
            return ((row * 2 + side) * 2 + core) * capacity + k

        jobs = []
        at = 0
        for n, (m, side, core, parts) in enumerate(pieces):
            slot = slot_of(m, side, core)
            live = t_ref[HEAD + slots + slot] > 0
            block = t_ref[HEAD + slot]
            ratio = ratio_ref[t_ref[HEAD + 2 * slots + slot]]
            copies = []
            start = 0
            for part in parts:
                rows = part.shape[0]
                copies.append(
                    pltpu.make_async_copy(
                        sources[at], in_buf.at[n, pl.ds(start, rows)], in_sem.at[n, len(copies)]
                    )
                )
                start += rows
                at += 1
            out = pltpu.make_async_copy(out_buf.at[n], out_ref.at[block], out_sem.at[n])
            jobs.append((n, live, ratio, copies, out))

        for n, live, ratio, copies, out in jobs:

            @pl.when(live)
            def _(copies=copies):
                for copy in copies:
                    copy.start()

        for n, live, ratio, copies, out in jobs:

            @pl.when(live)
            def _(n=n, ratio=ratio, copies=copies, out=out):
                for copy in copies:
                    copy.wait()
                out_buf[n] = (in_buf[n].astype(jnp.float32) * ratio).astype(jnp.bfloat16)
                out.start()

        for n, live, ratio, copies, out in jobs:

            @pl.when(live)
            def _(out=out):
                out.wait()

    count = len(pieces)
    anywhere = pl.BlockSpec(memory_space=pl.ANY)
    smem = pl.BlockSpec(memory_space=pltpu.SMEM)
    return pl.pallas_call(
        kernel,
        in_specs=[smem, smem] + [anywhere] * (len(flat) + len(carried)),
        out_specs=anywhere,
        out_shape=jax.ShapeDtypeStruct(shape, jnp.bfloat16),
        scratch_shapes=[
            pltpu.VMEM((count, size, size), jnp.bfloat16),
            pltpu.VMEM((count, size, size), jnp.bfloat16),
            pltpu.SemaphoreType.DMA((count, 2)),
            pltpu.SemaphoreType.DMA((count,)),
        ],
        input_output_aliases={2 + len(flat): 0} if carried else {},
        name=f"place_updates_{k}",
    )(table, graft_ratio, *flat, *carried)


def solution(mesh):
    return jax.shard_map(
        on_device,
        mesh=mesh,
        in_specs=(
            P("dp", "shard", None, None),
            P("shard", None),
            P(),
            P("dp", "shard", None, None),
            P("dp", "shard", None, None),
            P("dp", "shard", None, None),
            P("dp", "shard", None, None),
            P("dp", "shard", None, None),
        ),
        out_specs=(
            P("dp", "shard", None, None),
            P("dp", "shard", None, None),
            P("dp", "shard", None, None),
            P("shard", None, None),
        ),
        check_vma=False,
    )
```

```python
import jax
import jax.numpy as jnp
from jax import lax
from jax.experimental import pallas as pl
from jax.experimental.pallas import tpu as pltpu
from jax.sharding import PartitionSpec as P

NPARAM = 7

decay_rate = 0.95
tiny_value = 1e-06

HEAD = 8
GRANT = pltpu.CompilerParams(vmem_limit_bytes=4 * 1024 * 1024)
LARGE_GRANT = pltpu.CompilerParams(vmem_limit_bytes=12 * 1024 * 1024)

SMEM = pl.BlockSpec(memory_space=pltpu.SMEM)
VMEM = pl.BlockSpec(memory_space=pltpu.VMEM)
ANY = pl.BlockSpec(memory_space=pl.ANY)


def near(array):
    return pltpu.with_memory_space_constraint(array, pltpu.VMEM)


def far_off(array):
    return pltpu.with_memory_space_constraint(array, pltpu.HBM)


def wide(x):
    return x.astype(jnp.float32)


def slot_at(t, lines, m, side, core, capacity, k):
    row = lax.rem(t[0] + m, lines)
    return ((row * 2 + (t[1] ^ side)) * 2 + (t[2] ^ core)) * capacity + k


def first_pack(owner_row, params, me, grads, slots, capacity, lines):
    blocks, size, _ = grads.shape

    def kernel(owner_ref, param_ref, me_ref, grads_ref, out_ref, pack_ref, count_ref, sem):
        device = me_ref[0]
        first = me_ref[1] * blocks
        out_ref[0] = device // 4
        out_ref[1] = (device // 2) % 2
        out_ref[2] = device % 2
        for s in range(3 * slots):
            out_ref[HEAD + s] = 0
        for s in range(slots // capacity):
            count_ref[s] = 0
        for b in range(blocks):
            owner = owner_ref[b]
            place = owner * capacity + count_ref[owner]
            count_ref[owner] = count_ref[owner] + 1
            out_ref[HEAD + place] = b
            out_ref[HEAD + slots + place] = 1
            out_ref[HEAD + 2 * slots + place] = param_ref[first + b]
        copy_blocks(out_ref, grads_ref, [(pack_ref, 1, 0)], sem, lines, capacity)

    return pl.pallas_call(
        kernel,
        in_specs=[SMEM, SMEM, SMEM, ANY],
        out_specs=[SMEM, VMEM],
        out_shape=[
            jax.ShapeDtypeStruct((HEAD + 3 * slots,), jnp.int32),
            pltpu.VMEM((2 * lines, size, size), grads.dtype),
        ],
        scratch_shapes=[
            pltpu.SMEM((slots // capacity,), jnp.int32),
            pltpu.SemaphoreType.DMA((2 * lines,)),
        ],
        compiler_params=GRANT,
        name="first_pack",
    )(far_off(owner_row), far_off(params), me, far_off(grads))


def copy_blocks(t_ref, grads_ref, packs, sem, lines, capacity):
    copies = []
    for pack_ref, core, k in packs:
        for m in range(lines):
            for side in range(2):
                block = t_ref[HEAD + slot_at(t_ref, lines, m, side, core, capacity, k)]
                copies.append(
                    pltpu.make_async_copy(
                        grads_ref.at[block], pack_ref.at[m * 2 + side], sem.at[len(copies)]
                    )
                )
    for copy in copies:
        copy.start()
    for copy in copies:
        copy.wait()


def more_packs(table, grads, which, capacity, lines):
    size = grads.shape[-1]

    def kernel(t_ref, grads_ref, *refs):
        packs = [(ref, core, k) for ref, (core, k) in zip(refs, which)]
        copy_blocks(t_ref, grads_ref, packs, refs[-1], lines, capacity)

    return pl.pallas_call(
        kernel,
        in_specs=[SMEM, ANY],
        out_specs=[VMEM] * len(which),
        out_shape=[pltpu.VMEM((2 * lines, size, size), grads.dtype) for _ in which],
        scratch_shapes=[pltpu.SemaphoreType.DMA((2 * lines * len(which),))],
        compiler_params=GRANT,
        name="more_packs",
    )(table, far_off(grads))


def first_parts(own, got, lines, name):
    size = own.shape[-1]
    half = size // 2

    def kernel(own_ref, got_ref, side_ref, *row_refs):
        for m in range(lines):
            j = m * 2 + 1
            side_ref[m] = (wide(own_ref[j, :half]) + wide(got_ref[j, :half])).astype(jnp.bfloat16)
        for m in range(1, lines):
            for s in range(2):
                j = m * 2 + s
                row_refs[m - 1][s] = (wide(own_ref[j, half:]) + wide(got_ref[j, half:])).astype(
                    jnp.bfloat16
                )

    outs = pl.pallas_call(
        kernel,
        in_specs=[VMEM, VMEM],
        out_specs=[VMEM] * lines,
        out_shape=[pltpu.VMEM((lines, half, size), jnp.bfloat16)]
        + [pltpu.VMEM((2, half, size), jnp.bfloat16)] * (lines - 1),
        compiler_params=GRANT,
        name=name,
    )(near(own), near(got))
    return outs[0], list(outs[1:])


def second_parts(own, got, from_side, from_rows, lines, name):
    size = own.shape[-1]
    half = size // 2

    def kernel(own_ref, got_ref, side_in, *refs):
        rows_in = refs[: lines - 1]
        rows_out = refs[lines - 1 : 2 * lines - 2]
        side_out = refs[2 * lines - 2]
        for m in range(1, lines):
            j = m * 2
            rows_out[m - 1][...] = (
                wide(own_ref[j, :half]) + wide(got_ref[j, :half]) + wide(side_in[m])
            ).astype(jnp.bfloat16)
        total = wide(own_ref[1, half:]) + wide(got_ref[1, half:])
        for ref in rows_in:
            total = total + wide(ref[1])
        side_out[...] = total.astype(jnp.bfloat16)

    outs = pl.pallas_call(
        kernel,
        in_specs=[VMEM] * (2 + lines),
        out_specs=[VMEM] * lines,
        out_shape=[pltpu.VMEM((half, size), jnp.bfloat16)] * lines,
        compiler_params=GRANT,
        name=name,
    )(near(own), near(got), near(from_side), *[near(x) for x in from_rows])
    return list(outs[:-1]), outs[-1]


def owned_direction(k, table, own, got, from_side, from_rows, rest_rows, rest_side, left_root, right_root, slots, lines):
    capacity = left_root.shape[0]
    size = own.shape[-1]
    half = size // 2
    hops = lines - 1

    def kernel(t_ref, own_ref, got_ref, side_ref, *refs):
        rows_in = refs[:hops]
        rows_rest = refs[hops : 2 * hops]
        side_rest, left_ref, right_ref, direction_ref, held_ref, square_ref = refs[2 * hops :]
        live = t_ref[HEAD + slots + slot_at(t_ref, lines, 0, 0, 0, capacity, k)] > 0
        top = wide(own_ref[0, :half]) + wide(got_ref[0, :half]) + wide(side_ref[0])
        for ref in rows_rest:
            top = top + wide(ref[...])
        end = wide(own_ref[0, half:]) + wide(got_ref[0, half:]) + wide(side_rest[...])
        for ref in rows_in:
            end = end + wide(ref[0])
        summed = jnp.concatenate([top, end], axis=0)
        summed = jnp.where(live, summed, 0.0)
        held_ref[...] = summed
        left_half = jnp.dot(
            left_ref[k, 0], summed.astype(jnp.bfloat16), preferred_element_type=jnp.float32
        ).astype(jnp.bfloat16)
        direction = jnp.dot(left_half, right_ref[k, 0], preferred_element_type=jnp.float32)
        direction_ref[...] = direction.astype(jnp.bfloat16)
        square_ref[...] = jnp.sum((direction * direction).reshape(size // 8, 8, size), axis=0)

    return pl.pallas_call(
        kernel,
        in_specs=[SMEM] + [VMEM] * (6 + 2 * hops),
        out_specs=[VMEM] * 3,
        out_shape=[
            pltpu.VMEM((size, size), jnp.bfloat16),
            pltpu.VMEM((size, size), jnp.float32),
            pltpu.VMEM((8, size), jnp.float32),
        ],
        compiler_params=LARGE_GRANT,
        name=f"owned_direction_{k}",
    )(
        table,
        near(own),
        near(got),
        near(from_side),
        *[near(x) for x in from_rows],
        *[near(x) for x in rest_rows],
        near(rest_side),
        near(left_root),
        near(right_root),
    )


def owned_norms(table, helds, squares, moment, slots, lines):
    capacity = len(helds)
    size = moment.shape[-1]

    def kernel(t_ref, *refs):
        held_refs = refs[:capacity]
        square_refs = refs[capacity : 2 * capacity]
        moment_ref, moment_out, tile_ref = refs[2 * capacity :]
        row = lax.broadcasted_iota(jnp.int32, (8, 128), 0)
        lane = lax.broadcasted_iota(jnp.int32, (8, 128), 1)
        tile = jnp.zeros((8, 128), jnp.float32)
        for k in range(capacity):
            slot = slot_at(t_ref, lines, 0, 0, 0, capacity, k)
            live = t_ref[HEAD + slots + slot] > 0
            param = t_ref[HEAD + 2 * slots + slot]
            held = held_refs[k][...]
            fresh = decay_rate * moment_ref[k, 0] + (1.0 - decay_rate) * (held * held)
            moment_out[k, 0] = fresh
            adam = held / (jnp.sqrt(fresh) + tiny_value)
            adam_square = jnp.sum(adam * adam)
            direction_square = jnp.sum(square_refs[k][...])
            value = jnp.where(lane == 0, adam_square, jnp.where(lane == 1, direction_square, 0.0))
            tile = tile + jnp.where((row == param) & live, value, 0.0)
        tile_ref[...] = tile

    return pl.pallas_call(
        kernel,
        in_specs=[SMEM] + [VMEM] * (2 * capacity + 1),
        out_specs=[VMEM, VMEM],
        out_shape=[
            jax.ShapeDtypeStruct(moment.shape, jnp.float32),
            pltpu.VMEM((8, 128), jnp.float32),
        ],
        compiler_params=LARGE_GRANT,
        name="owned_norms",
    )(table, *[near(x) for x in helds], *[near(x) for x in squares], near(moment))


def place_updates(k, capacity, slots, lines, table, ratios, pieces, update, shape, name):
    size = shape[-1]
    flat = [part for _, _, _, parts in pieces for part in parts]
    carried = [] if update is None else [update]

    def kernel(t_ref, ratio_ref, *refs):
        sources = refs[: len(flat)]
        out_ref, buf, sem = refs[len(flat) + len(carried) :]

        at = 0
        jobs = []
        for n, (m, side, core, parts) in enumerate(pieces):
            slot = slot_at(t_ref, lines, lines - m, side, core, capacity, k)
            live = t_ref[HEAD + slots + slot] > 0
            ratio = ratio_ref[t_ref[HEAD + 2 * slots + slot]]
            out = pltpu.make_async_copy(buf.at[n], out_ref.at[t_ref[HEAD + slot]], sem.at[n])
            here = sources[at : at + len(parts)]
            at += len(parts)
            jobs.append((live, out))

            @pl.when(live)
            def _(n=n, ratio=ratio, here=here, out=out):
                start = 0
                for ref in here:
                    rows = ref.shape[0]
                    buf[n, start : start + rows] = (wide(ref[...]) * ratio).astype(jnp.bfloat16)
                    start += rows
                out.start()

        for live, out in jobs:

            @pl.when(live)
            def _(out=out):
                out.wait()

    count = len(pieces)
    return pl.pallas_call(
        kernel,
        in_specs=[SMEM, SMEM] + [VMEM] * len(flat) + [ANY] * len(carried),
        out_specs=ANY,
        out_shape=jax.ShapeDtypeStruct(shape, jnp.bfloat16),
        scratch_shapes=[
            pltpu.VMEM((count, size, size), jnp.bfloat16),
            pltpu.SemaphoreType.DMA((count,)),
        ],
        input_output_aliases={2 + len(flat): 0} if carried else {},
        compiler_params=LARGE_GRANT,
        name=name,
    )(table, ratios, *[near(x) for x in flat], *carried)


def on_device(gradients, owners, block_param, left_stat, right_stat, moment, left_root, right_root):
    replicas = lax.axis_size("dp")
    capacity = left_stat.shape[0]
    size = gradients.shape[3]
    half = size // 2
    grads = gradients[0]
    blocks = grads.shape[0]
    slots = replicas * capacity
    lines = replicas // 4
    hops = range(1, lines)

    by_core = [(i, i ^ 1) for i in range(replicas)]
    by_side = [(i, i ^ 2) for i in range(replicas)]

    def by_row(m):
        return [(i, (i + 4 * m) % replicas) for i in range(replicas)]

    def send(array, perm):
        return lax.ppermute(array, "dp", perm)

    me = jnp.stack([lax.axis_index("dp"), lax.axis_index("shard")]).astype(jnp.int32)
    table, pack = first_pack(owners[0], block_param, me, grads, slots, capacity, lines)
    which = [(1, k) for k in range(1, capacity)] + [(0, k) for k in range(capacity)]
    packs = more_packs(table, grads, which, capacity, lines)
    own = packs[capacity - 1 :]
    got = [send(x, by_core) for x in [pack] + list(packs[: capacity - 1])]

    from_side, from_rows = [], []
    for k in range(capacity):
        side_part, row_parts = first_parts(own[k], got[k], lines, f"first_parts_{k}")
        from_side.append(send(side_part, by_side))
        from_rows.append([send(row_parts[m - 1], by_row(m)) for m in hops])
    rest_rows, rest_side = [], []
    for k in range(capacity):
        row_parts, side_part = second_parts(
            own[k], got[k], from_side[k], from_rows[k], lines, f"second_parts_{k}"
        )
        rest_rows.append([send(row_parts[m - 1], by_row(m)) for m in hops])
        rest_side.append(send(side_part, by_side))
    directions, helds, squares = [], [], []
    for k in range(capacity):
        direction, held, square = owned_direction(
            k,
            table,
            own[k],
            got[k],
            from_side[k],
            from_rows[k],
            rest_rows[k],
            rest_side[k],
            left_root,
            right_root,
            slots,
            lines,
        )
        directions.append(direction)
        helds.append(held)
        squares.append(square)

    new_moment, norms = owned_norms(table, helds, squares, moment, slots, lines)
    columns = lax.axis_size("shard")
    total = norms
    for shift in range(1, columns):
        total = total + lax.ppermute(
            norms, "shard", [(i, (i + shift) % columns) for i in range(columns)]
        )
    total = total + send(total, by_core)
    total = total + send(total, by_side)
    part = total
    for m in hops:
        total = total + send(part, by_row(m))
    ratios = jnp.sqrt((total[:, 0] + tiny_value) / (total[:, 1] + tiny_value))

    close, far = [], []
    for k in range(capacity):
        mine = directions[k]
        by_s = send(mine, by_side)
        by_r = [send(mine, by_row(m)) for m in hops]
        far_top = [send(by_s[:half], by_row(m)) for m in hops]
        far_end = [send(array[half:], by_side) for array in by_r]
        first = [(0, 0, (mine,)), (0, 1, (by_s,))] + [(m, 0, (by_r[m - 1],)) for m in hops]
        last = [(m, 1, (far_top[m - 1], far_end[m - 1])) for m in hops]
        for pieces, bucket in ((first, close), (last, far)):
            bucket.append(
                [(m, side, 0, parts) for m, side, parts in pieces]
                + [
                    (m, side, 1, tuple(send(part, by_core) for part in parts))
                    for m, side, parts in pieces
                ]
            )

    held = jnp.stack(helds)
    left_gram = jnp.einsum("cij,ckj->cik", held, held, precision=lax.Precision.HIGHEST)
    right_gram = jnp.einsum("cji,cjk->cik", held, held, precision=lax.Precision.HIGHEST)
    new_left = decay_rate * left_stat + (1.0 - decay_rate) * left_gram[:, None]
    new_right = decay_rate * right_stat + (1.0 - decay_rate) * right_gram[:, None]

    update = None
    for group, pieces in (("close", close), ("far", far)):
        for k in range(capacity):
            update = place_updates(
                k,
                capacity,
                slots,
                lines,
                table,
                ratios,
                pieces[k],
                update,
                (blocks, size, size),
                f"place_{group}_{k}",
            )
    return (new_left, new_right, new_moment, update)


def solution(mesh):
    return jax.shard_map(
        on_device,
        mesh=mesh,
        in_specs=(
            P("dp", "shard", None, None),
            P("shard", None),
            P(),
            P("dp", "shard", None, None),
            P("dp", "shard", None, None),
            P("dp", "shard", None, None),
            P("dp", "shard", None, None),
            P("dp", "shard", None, None),
        ),
        out_specs=(
            P("dp", "shard", None, None),
            P("dp", "shard", None, None),
            P("dp", "shard", None, None),
            P("shard", None, None),
        ),
        check_vma=False,
    )
```
